256 devices in a mesh: beam: 32 (over z_lo, x, core), tm: 8 (over z_hi, y).
Axes of the slice: x: 4, y: 4, z: 8 (z_hi: 2, z_lo: 4; z = z_hi * 4 + z_lo), core: 2. Of those that a mesh axis runs over, the one named last changes fastest.
Arguments:
- spectra: bfloat16 [1024, 128, 2, 2048], P('beam', 'tm'), may hold values from -6 to 6
- steering: bfloat16 [32, 2, 512, 1024], P('beam'), may hold values from -0.125 to 0.125
- templates: bfloat16 [256, 8, 2048], P(None, None, 'beam'), may hold values from -0.046875 to 0.046875
- tmpl_length: int32 [256], replicated, may hold values from 1 to 8
- band_start: int32 [256], replicated, may hold values from 0 to 1023
- band_width: int32 [256], replicated, may hold values from 256 to 1024
Outputs:
- scores: float32 [512, 128, 256], P('beam', 'tm')
The draws below stay inside these ranges and needn't reach their ends.
Inputs may be any that keep to these rules, and one draw needn't show every extreme that they name: `tmpl_length`: lengths of templates in frames. band_start + band_width <= 2048.
All inputs are finite; a program needn't handle non-finite values.
Results may differ from the reference program's by a relative error of at most 0.0029.
Values may be sent and summed in bfloat16 or wider, within the bound.
A program may use at most 128 MiB of HBM per device.

```python
import jax
import jax.numpy as jnp
from jax import lax

C = 1024
K = 2048
B = 512
M = 256
SUB_BINS = 64
LAG = 8
FRAMES = 128
NSUB = 32


def set_ends(drawn, key, smallest, top_value):
    dims = drawn.shape
    spot = [jax.random.randint(jax.random.fold_in(key, axis), (), 0, dims[axis]) for axis in range(len(dims))]
    drawn = drawn.at[tuple(spot)].set(smallest)
    longest = dims.index(max(dims))
    spot[longest] = (spot[longest] + 1) % dims[longest]
    return drawn.at[tuple(spot)].set(top_value)


def levels(own_key, extent, shards, least, top_value):
    factor_of = 1.0
    for dim, shards_of in shards:
        heights = jax.random.uniform(jax.random.fold_in(jax.random.fold_in(own_key, 6), dim), (shards_of,), jnp.float32, least / len(shards), top_value / len(shards))
        factor_of = factor_of * jnp.repeat(jnp.exp(heights), extent[dim] // shards_of).reshape((-1,) + (1,) * (len(extent) - 1 - dim))
    return factor_of


def bell_draw(rng, dims, scale, most, cuts=(), kind=jnp.bfloat16):
    result = jax.random.normal(rng, dims, jnp.float32) * scale
    if len(cuts) > 0:
        result = levels(rng, dims, cuts, -0.22, 0.18) * result
    return jnp.clip(result, min=-most, max=most).astype(kind)


def setup_inputs(seed: int = 0) -> dict:
    keys = jax.random.split(jax.random.key(seed), 7)
    spectra = bell_draw(keys[0], (C, FRAMES, 2, K), 1.0, 6.0, ((0, 32), (1, 8)))
    steering = bell_draw(keys[1], (NSUB, 2, B, C), (2 * C) ** -0.5, 0.125, ((0, 32),))
    templates = bell_draw(keys[2], (M, LAG, K), (LAG * K) ** -0.5, 0.046875, ((2, 32),))
    tmpl_length = set_ends(jax.random.randint(keys[3], (M,), 1, LAG + 1), jax.random.fold_in(keys[3], 1), 1, LAG).astype(jnp.int32)
    band_start = set_ends(jax.random.randint(keys[4], (M,), 0, K // 2), jax.random.fold_in(keys[4], 1), 0, (K // 2) - 1).astype(jnp.int32)
    band_width = set_ends(jax.random.randint(keys[5], (M,), K // 8, K // 2 + 1), jax.random.fold_in(keys[5], 1), K // 8, (K // 2 + 1) - 1).astype(jnp.int32)
    return {"spectra": spectra, "steering": steering, "templates": templates, "tmpl_length": tmpl_length, "band_start": band_start, "band_width": band_width}


def masked_templates(templates, tmpl_length, band_start, band_width, first_bin):
    lag_count = templates.shape[1]
    bin_count = templates.shape[2]
    lag_index = jnp.arange(lag_count, dtype=jnp.int32)
    bin_index = first_bin + jnp.arange(bin_count, dtype=jnp.int32)
    lag_keep = lag_index[None, :, None] < tmpl_length[:, None, None]
    band_end = band_start + band_width
    band_keep = (bin_index[None, None, :] >= band_start[:, None, None]) & (bin_index[None, None, :] < band_end[:, None, None])
    return jnp.where(lag_keep & band_keep, templates, jnp.zeros_like(templates))


def reference(spectra, steering, templates, tmpl_length, band_start, band_width):
    channels = spectra.shape[0]
    frames = spectra.shape[1]
    bin_total = spectra.shape[3]

    def subband(index):
        section = lax.dynamic_slice_in_dim(spectra, index * SUB_BINS, SUB_BINS, 3)
        real_part = section[:, :, 0].reshape(channels, frames * SUB_BINS)
        imag_part = section[:, :, 1].reshape(channels, frames * SUB_BINS)
        weights = steering[index]
        beam_real = jnp.dot(weights[0], real_part, preferred_element_type=jnp.float32) - jnp.dot(weights[1], imag_part, preferred_element_type=jnp.float32)
        beam_imag = jnp.dot(weights[0], imag_part, preferred_element_type=jnp.float32) + jnp.dot(weights[1], real_part, preferred_element_type=jnp.float32)
        squared = beam_real * beam_real + beam_imag * beam_imag
        return squared.astype(jnp.bfloat16).reshape(B, frames, SUB_BINS)

    stacked = lax.map(subband, jnp.arange(NSUB, dtype=jnp.int32))
    beam_power = jnp.transpose(stacked, (1, 2, 0, 3)).reshape(B, frames, bin_total)
    weights = masked_templates(templates, tmpl_length, band_start, band_width, jnp.int32(0))
    extended = jnp.concatenate([beam_power, jnp.zeros((B, LAG - 1, bin_total), jnp.bfloat16)], axis=1)
    scores = jnp.zeros((B * frames, M), jnp.float32)
    for offset in range(LAG):
        slab = extended[:, offset:offset + frames, :].reshape(B * frames, bin_total)
        scores = scores + jnp.dot(slab, weights[:, offset, :].T, preferred_element_type=jnp.float32)
    return scores.reshape(B, frames, M)
```

```python
import jax
import jax.numpy as jnp
from jax import lax
from jax.experimental import pallas as pl
from jax.experimental.pallas import tpu as pltpu
from jax.sharding import PartitionSpec as P

MESH = pl.DeviceIdType.MESH
CHUNKS = 4
LAGS = 8
F32 = jnp.float32
BF16 = jnp.bfloat16


def kernel(
    spec, steer, tmpl, tlen, bst, bwd, out,
    xbuf, wst, wmix, ppow, pin, tbuf, acc, sbuf, hsend, hrecv,
    w_own, w_send, w_recv, x_own, x_send, x_recv, t_send, t_recv, t2_send, t2_recv,
    p_own, p_send, p_recv, s_send, s_recv, h_send, h_recv,
):
    me = lax.axis_index("beam")
    tm = lax.axis_index("tm")
    core = me % 2
    sib = me + 1 - 2 * core
    chip = me // 2
    half = me // 16
    local = me % 16
    kk = local // 2
    partner = (me + 16) % 32

    def remote(src, dst, send_sem, recv_sem, beam, tm_index=None):
        return pltpu.make_async_remote_copy(
            src_ref=src, dst_ref=dst, send_sem=send_sem, recv_sem=recv_sem,
            device_id=(beam, tm if tm_index is None else tm_index), device_id_type=MESH,
        )

    def tile(device):
        return pl.ds(pl.multiple_of((device // 2) * 128, 128), 128)

    own_w = pltpu.make_async_copy(steer.at[0], wst.at[core], w_own)
    own_w.start()

    def own_x(g, _):
        pltpu.make_async_copy(
            spec.at[:, 4 * (g // 2) + 2 * core + g % 2, :, tile(me)],
            xbuf.at[g, pl.ds(32 * me, 32)], x_own,
        ).start()
        return 0

    lax.fori_loop(0, 8, own_x, 0)

    bins = 64 * me + lax.broadcasted_iota(jnp.int32, (64, 256), 0)
    first = bst[...]
    keep = jnp.where((bins >= first) & (bins < first + bwd[...]), 1, 0)
    length = jnp.broadcast_to(tlen[...], (64, 256))
    for lag in range(LAGS):
        tbuf[lag, kk, core] = jnp.where(
            (keep == 1) & (length > lag), tmpl[lag].astype(F32), 0.0
        ).astype(BF16)

    barrier = pltpu.get_barrier_semaphore()

    def greet(off, _):
        pl.semaphore_signal(barrier, inc=1, device_id=((me + off) % 32, tm), device_id_type=MESH)
        return 0

    lax.fori_loop(1, 32, greet, 0)
    for d in (1, 7):
        pl.semaphore_signal(barrier, inc=1, device_id=(me, (tm + d) % 8), device_id_type=MESH)
    pl.semaphore_wait(barrier, 33)

    w_copy = remote(steer.at[0], wst.at[core], w_send, w_recv, sib)
    w_copy.start()

    def send_x(j):
        def body(off, _):
            peer = (me + off) % 32
            for i in range(2):
                remote(
                    spec.at[:, 4 * j + 2 * (peer % 2) + i, :, tile(peer)],
                    xbuf.at[2 * j + i, pl.ds(32 * me, 32)],
                    x_send.at[j], x_recv.at[j], peer,
                ).start()
            return 0

        lax.fori_loop(1, 32, body, 0)

    send_x(0)

    def send_t(off, _):
        peer = 16 * half + (local + 2 * off) % 16
        remote(
            tbuf.at[:, kk, core], tbuf.at[:, kk, core], t_send, t_recv, peer
        ).start()
        return 0

    lax.fori_loop(1, 8, send_t, 0)
    send_x(1)

    own_w.wait()
    w_copy.wait_recv()
    row = lax.broadcasted_iota(jnp.int32, (256, 256), 0)
    col = lax.broadcasted_iota(jnp.int32, (256, 256), 1)
    e_even = jnp.where((row < 128) & (col == 2 * row), 1.0, 0.0)
    odd = (row >= 128) & (col == 2 * (row - 128) + 1)
    e_real = (e_even - jnp.where(odd, 1.0, 0.0)).astype(BF16)
    i_even = (row >= 128) & (col == 2 * (row - 128))
    i_odd = (row < 128) & (col == 2 * row + 1)
    e_imag = jnp.where(i_even | i_odd, 1.0, 0.0).astype(BF16)

    def mix(n, _):
        s, cb = n // 8, n % 8
        cols = pl.ds(pl.multiple_of(cb * 128, 128), 128)
        both = jnp.concatenate([wst[s, 0, :, cols], wst[s, 1, :, cols]], axis=1)
        outcols = pl.ds(pl.multiple_of(cb * 256, 256), 256)
        for ri, e in enumerate((e_real, e_imag)):
            m = jnp.dot(both, e, preferred_element_type=F32).astype(BF16)
            rows = pl.ds(pl.multiple_of((s * 2 + ri) * 128, 128), 128)
            wmix[:, rows, outcols] = m.reshape(4, 128, 256)
        return 0

    lax.fori_loop(0, 16, mix, 0)
    acc[...] = jnp.zeros_like(acc)

    xflat = xbuf.reshape(8, 2048, 128)
    lane = lax.broadcasted_iota(jnp.int32, (128, 256), 1)
    low = lane % 128 < 64

    def power(j):
        pltpu.make_async_copy(
            xbuf.at[pl.ds(0, 2), pl.ds(0, 992)], xbuf.at[pl.ds(0, 2), pl.ds(0, 992)], x_recv.at[j]
        ).wait()

        def block(b, _):
            x = jnp.concatenate([xflat[2 * j], xflat[2 * j + 1]], axis=1)
            y = jnp.dot(wmix[b], x, preferred_element_type=F32)
            ar, ai, br, bi = y[0:128], y[128:256], y[256:384], y[384:512]
            p = jnp.where(low, ar * ar + ai * ai, br * br + bi * bi).astype(BF16)
            for f in range(2):
                ppow[j, f, b // 2, b % 2] = p[:, f * 128 : (f + 1) * 128].reshape(8, 16, 128)
            return 0

        lax.fori_loop(0, 4, block, 0)

        pltpu.make_async_copy(
            ppow.at[j, :, :, local // 8, local % 8], pin.at[j, core, :, :, kk], p_own.at[j]
        ).start()

        def send_p(off, _):
            q = (local + off) % 16
            remote(
                ppow.at[j, :, :, q // 8, q % 8], pin.at[j, core, :, :, kk],
                p_send.at[j], p_recv.at[j], 16 * half + q,
            ).start()
            return 0

        lax.fori_loop(1, 16, send_p, 0)

    def seg(j):
        return (4 * j, 4) if j < CHUNKS - 1 else (12, 11)

    def score_copy(j):
        t0, n = seg(j)
        return remote(
            acc.at[pl.ds(t0, n), 1 - half], sbuf.at[pl.ds(t0, n)], s_send.at[j], s_recv.at[j], partner
        )

    def correlate(j):
        pltpu.make_async_copy(
            ppow.at[j, :, :, local // 8, local % 8], pin.at[j, core, :, :, kk], p_own.at[j]
        ).wait()
        wait_p(j)

        def lag_step(lag, _):
            parts = [pin[j, :, :, :, k].reshape(128, 128) for k in range(8)]
            lhs = jnp.concatenate(parts, axis=1)
            w = tbuf[lag].reshape(1024, 256)
            res = jnp.dot(lhs, w, preferred_element_type=F32).reshape(4, 2, 16, 256)
            rows = pl.ds(4 * j + 7 - lag, 4)
            acc[rows] = acc[rows] + res
            return 0

        lax.fori_loop(0, LAGS, lag_step, 0)
        score_copy(j).start()

    def wait_p(j):
        d = xbuf.at[0, pl.ds(0, 480)]
        pltpu.make_async_copy(d, d, p_recv.at[j]).wait()

    d = xbuf.at[pl.ds(0, 8), pl.ds(0, 32)]
    pltpu.make_async_copy(d, d, x_own).wait()
    power(0)
    send_x(2)
    d = tbuf.at[:, pl.ds(0, 7), 0]
    pltpu.make_async_copy(d, d, t_recv).wait()
    t2 = remote(tbuf.at[:, :, core], tbuf.at[:, :, core], t2_send, t2_recv, sib)
    t2.start()
    power(1)
    send_x(3)
    t2.wait_recv()
    correlate(0)
    power(2)
    correlate(1)
    power(3)
    correlate(2)

    score_copy(0).wait_recv()
    score_copy(1).wait_recv()
    h_copy = remote(hsend, hrecv, h_send, h_recv, me, (tm + 7) % 8)

    @pl.when(tm > 0)
    def _():
        hsend[...] = acc[0:7, half] + sbuf[0:7]
        h_copy.start()

    correlate(3)
    score_copy(2).wait_recv()
    score_copy(3).wait_recv()
    out[...] = acc[7:23, half] + sbuf[7:23]

    @pl.when(tm < 7)
    def _():
        h_copy.wait_recv()
        out[9:16] = out[9:16] + hrecv[...]

    w_copy.wait_send()
    t2.wait_send()
    d = tbuf.at[:, pl.ds(0, 7), 0]
    pltpu.make_async_copy(d, d, t_send).wait()
    for j in range(CHUNKS):
        d = xbuf.at[pl.ds(0, 2), pl.ds(0, 992)]
        pltpu.make_async_copy(d, d, x_send.at[j]).wait()
        d = xbuf.at[0, pl.ds(0, 480)]
        pltpu.make_async_copy(d, d, p_send.at[j]).wait()
        score_copy(j).wait_send()

    @pl.when(tm > 0)
    def _():
        h_copy.wait_send()


def per_device(spectra, steering, templates, tmpl_length, band_start, band_width):
    rows = [a.reshape(1, -1) for a in (tmpl_length, band_start, band_width)]
    by_bin = jnp.transpose(templates, (1, 2, 0))
    any_spec = pl.BlockSpec(memory_space=pl.ANY)
    vmem = pl.BlockSpec(memory_space=pltpu.VMEM)
    dma = pltpu.SemaphoreType.DMA
    scores = pl.pallas_call(
        kernel,
        out_shape=jax.ShapeDtypeStruct((16, 16, 256), F32),
        in_specs=[any_spec, any_spec, vmem, vmem, vmem, vmem],
        out_specs=vmem,
        scratch_shapes=[
            pltpu.VMEM((8, 1024, 2, 128), BF16),
            pltpu.VMEM((2, 2, 512, 1024), BF16),
            pltpu.VMEM((4, 512, 2048), BF16),
            pltpu.VMEM((4, 2, 2, 2, 8, 16, 128), BF16),
            pltpu.VMEM((4, 2, 2, 2, 8, 16, 128), BF16),
            pltpu.VMEM((8, 8, 2, 64, 256), BF16),
            pltpu.VMEM((23, 2, 16, 256), F32),
            pltpu.VMEM((23, 16, 256), F32),
            pltpu.VMEM((7, 16, 256), F32),
            pltpu.VMEM((7, 16, 256), F32),
            dma(()), dma(()), dma(()),
            dma(()), dma((4,)), dma((4,)),
            dma(()), dma(()), dma(()), dma(()),
            dma((4,)), dma((4,)), dma((4,)),
            dma((4,)), dma((4,)), dma(()), dma(()),
        ],
        compiler_params=pltpu.CompilerParams(
            collective_id=0, has_side_effects=True, vmem_limit_bytes=56 * 1024 * 1024
        ),
    )(spectra, steering, by_bin, *rows)
    return jnp.transpose(scores, (1, 0, 2))


def solution(mesh):
    return jax.shard_map(
        per_device,
        mesh=mesh,
        in_specs=(
            P("beam", "tm", None, None),
            P("beam", None, None, None),
            P(None, None, "beam"),
            P(),
            P(),
            P(),
        ),
        out_specs=P("beam", "tm", None),
        check_vma=False,
    )
```

```python
import jax
import jax.numpy as jnp
from jax import lax
from jax.experimental import pallas as pl
from jax.experimental.pallas import tpu as pltpu
from jax.sharding import PartitionSpec as P

MESH = pl.DeviceIdType.MESH
CHUNKS = 8
LAGS = 8
SEGMENTS = ((0, 8), (8, 6), (14, 9))
F32 = jnp.float32
BF16 = jnp.bfloat16
SENT = BF16


def kernel(
    spec, steer, tmpl, tlen, bst, bwd, out,
    xbuf, wst, wmix, ppow, pin, tbuf, acc, ssend, sbuf, hsend, hrecv,
    w_own, w_send, w_recv, x_own, x_send, x_recv, t_send, t_recv, y_send, y_recv, t2_send, t2_recv,
    p_own, p_send, p_recv, s_send, s_recv, h_send, h_recv,
):
    me = lax.axis_index("beam")
    tm = lax.axis_index("tm")
    core = me % 2
    sib = me + 1 - 2 * core
    half = me // 16
    local = me % 16
    kk = local // 2
    partner = (me + 16) % 32
    quarter = tm % 4

    def remote(src, dst, send_sem, recv_sem, beam, tm_index=None):
        return pltpu.make_async_remote_copy(
            src_ref=src, dst_ref=dst, send_sem=send_sem, recv_sem=recv_sem,
            device_id=(beam, tm if tm_index is None else tm_index), device_id_type=MESH,
        )

    def y_peer(off):
        return tm - quarter + (quarter + off) % 4

    def wait_bytes(ref, sem):
        pltpu.make_async_copy(ref, ref, sem).wait()

    def tile(device):
        return pl.ds(pl.multiple_of((device // 2) * 128, 128), 128)

    barrier = pltpu.get_barrier_semaphore()

    def greet(off, _):
        pl.semaphore_signal(barrier, inc=1, device_id=((me + off) % 32, tm), device_id_type=MESH)
        return 0

    lax.fori_loop(1, 32, greet, 0)
    for off in (1, 2, 3):
        pl.semaphore_signal(barrier, inc=1, device_id=(me, y_peer(off)), device_id_type=MESH)

    @pl.when((tm == 3) | (tm == 4))
    def _():
        pl.semaphore_signal(barrier, inc=1, device_id=(me, 7 - tm), device_id_type=MESH)

    own_w = pltpu.make_async_copy(steer.at[0], wst.at[core], w_own)
    own_w.start()

    def own_x(j, _):
        pltpu.make_async_copy(
            spec.at[:, 2 * j + core, :, tile(me)], xbuf.at[j, pl.ds(32 * me, 32)], x_own
        ).start()
        return 0

    lax.fori_loop(0, CHUNKS, own_x, 0)

    bins = 64 * me + lax.broadcasted_iota(jnp.int32, (64, 256), 0)
    first = bst[...]
    keep = jnp.where((bins >= first) & (bins < first + bwd[...]), 1, 0)
    length = jnp.broadcast_to(tlen[...], (64, 256))
    for i in range(2):
        lag = 2 * quarter + i
        tbuf[lag, kk, core] = jnp.where(
            (keep == 1) & (length > lag), tmpl[lag].astype(F32), 0.0
        ).astype(BF16)

    pl.semaphore_wait(barrier, 34 + jnp.where((tm == 3) | (tm == 4), 1, 0))

    w_copy = remote(steer.at[0], wst.at[core], w_send, w_recv, sib)
    w_copy.start()

    def send_t(off, _):
        part = tbuf.at[pl.ds(2 * quarter, 2), kk, core]
        remote(part, part, t_send, t_recv, 16 * half + (local + 2 * off) % 16).start()
        return 0

    lax.fori_loop(1, 8, send_t, 0)

    def send_x(j):
        def body(off, _):
            peer = (me + off) % 32
            remote(
                spec.at[:, 2 * j + peer % 2, :, tile(peer)],
                xbuf.at[j, pl.ds(32 * me, 32)],
                x_send.at[j], x_recv.at[j], peer,
            ).start()
            return 0

        lax.fori_loop(1, 32, body, 0)

    send_x(0)
    send_x(1)

    own_w.wait()
    w_copy.wait_recv()
    row = lax.broadcasted_iota(jnp.int32, (256, 256), 0)
    col = lax.broadcasted_iota(jnp.int32, (256, 256), 1)
    e_even = jnp.where((row < 128) & (col == 2 * row), 1.0, 0.0)
    odd = (row >= 128) & (col == 2 * (row - 128) + 1)
    e_real = (e_even - jnp.where(odd, 1.0, 0.0)).astype(BF16)
    i_even = (row >= 128) & (col == 2 * (row - 128))
    i_odd = (row < 128) & (col == 2 * row + 1)
    e_imag = jnp.where(i_even | i_odd, 1.0, 0.0).astype(BF16)

    def mix(n, _):
        s, cb = n // 8, n % 8
        cols = pl.ds(pl.multiple_of(cb * 128, 128), 128)
        both = jnp.concatenate([wst[s, 0, :, cols], wst[s, 1, :, cols]], axis=1)
        outcols = pl.ds(pl.multiple_of(cb * 256, 256), 256)
        for ri, e in enumerate((e_real, e_imag)):
            m = jnp.dot(both, e, preferred_element_type=F32).astype(BF16)
            rows = pl.ds(pl.multiple_of((s * 2 + ri) * 128, 128), 128)
            wmix[:, rows, outcols] = m.reshape(4, 128, 256)
        return 0

    lax.fori_loop(0, 16, mix, 0)
    acc[...] = jnp.zeros_like(acc)

    wait_bytes(tbuf.at[pl.ds(0, 2), pl.ds(0, 7), 0], t_recv)
    for off in (1, 2, 3):
        part = tbuf.at[pl.ds(2 * quarter, 2), :, core]
        remote(part, part, y_send, y_recv, me, y_peer(off)).start()

    xflat = xbuf.reshape(CHUNKS, 2048, 128)
    low = lax.broadcasted_iota(jnp.int32, (128, 128), 1) < 64

    def own_p(j):
        return pltpu.make_async_copy(
            ppow.at[j, :, local // 8, local % 8], pin.at[j, core, :, kk], p_own.at[j]
        )

    def power(j):
        wait_bytes(xbuf.at[0, pl.ds(0, 992)], x_recv.at[j])

        def block(b, _):
            y = jnp.dot(wmix[b], xflat[j], preferred_element_type=F32)
            ar, ai, br, bi = y[0:128], y[128:256], y[256:384], y[384:512]
            p = jnp.where(low, ar * ar + ai * ai, br * br + bi * bi).astype(BF16)
            ppow[j, b // 2, b % 2] = p.reshape(8, 16, 128)
            return 0

        lax.fori_loop(0, 4, block, 0)
        own_p(j).start()

        def send_p(off, _):
            q = (local + off) % 16
            remote(
                ppow.at[j, :, q // 8, q % 8], pin.at[j, core, :, kk],
                p_send.at[j], p_recv.at[j], 16 * half + q,
            ).start()
            return 0

        lax.fori_loop(1, 16, send_p, 0)

    def correlate(j):
        own_p(j).wait()
        wait_bytes(xbuf.at[0, pl.ds(0, 240)], p_recv.at[j])

        def lag_step(lag, _):
            parts = [pin[j, :, :, k].reshape(64, 128) for k in range(8)]
            lhs = jnp.concatenate(parts, axis=1)
            w = tbuf[lag].reshape(1024, 256)
            res = jnp.dot(lhs, w, preferred_element_type=F32).reshape(2, 2, 16, 256)
            rows = pl.ds(2 * j + 7 - lag, 2)
            acc[rows] = acc[rows] + res
            return 0

        lax.fori_loop(0, LAGS, lag_step, 0)

    def score_copy(g):
        rows = pl.ds(*SEGMENTS[g])
        return remote(ssend.at[rows], sbuf.at[rows], s_send.at[g], s_recv.at[g], partner)

    def send_scores(g):
        rows = pl.ds(*SEGMENTS[g])
        ssend[rows] = acc[rows, 1 - half].astype(SENT)
        score_copy(g).start()

    t2 = remote(tbuf.at[:, :, core], tbuf.at[:, :, core], t2_send, t2_recv, sib)
    h_copy = remote(hsend, hrecv, h_send, h_recv, me, tm - 1)

    wait_bytes(xbuf.at[pl.ds(0, CHUNKS), pl.ds(0, 32)], x_own)
    power(0)
    send_x(2)
    power(1)
    send_x(3)
    power(2)
    send_x(4)
    wait_bytes(tbuf.at[pl.ds(0, 6), :, 0], y_recv)
    t2.start()
    power(3)
    send_x(5)
    t2.wait_recv()
    correlate(0)
    correlate(1)
    power(4)
    send_x(6)
    correlate(2)
    correlate(3)
    send_scores(0)
    power(5)
    send_x(7)
    correlate(4)
    power(6)
    correlate(5)

    score_copy(0).wait_recv()

    @pl.when(tm > 0)
    def _():
        hsend[...] = (acc[0:7, half] + sbuf[0:7].astype(F32)).astype(SENT)
        h_copy.start()

    power(7)
    correlate(6)
    send_scores(1)
    correlate(7)
    send_scores(2)
    score_copy(1).wait_recv()
    score_copy(2).wait_recv()
    out[...] = acc[7:23, half] + sbuf[7:23].astype(F32)

    @pl.when(tm < 7)
    def _():
        h_copy.wait_recv()
        out[9:16] = out[9:16] + hrecv[...].astype(F32)

    w_copy.wait_send()
    t2.wait_send()
    wait_bytes(tbuf.at[pl.ds(0, 2), pl.ds(0, 7), 0], t_send)
    wait_bytes(tbuf.at[pl.ds(0, 6), :, 0], y_send)
    for j in range(CHUNKS):
        wait_bytes(xbuf.at[0, pl.ds(0, 992)], x_send.at[j])
        wait_bytes(xbuf.at[0, pl.ds(0, 240)], p_send.at[j])
    for g in range(3):
        score_copy(g).wait_send()

    @pl.when(tm > 0)
    def _():
        h_copy.wait_send()


def per_device(spectra, steering, templates, tmpl_length, band_start, band_width):
    rows = [a.reshape(1, -1) for a in (tmpl_length, band_start, band_width)]
    by_bin = jnp.transpose(templates, (1, 2, 0))
    any_spec = pl.BlockSpec(memory_space=pl.ANY)
    vmem = pl.BlockSpec(memory_space=pltpu.VMEM)
    dma = pltpu.SemaphoreType.DMA
    scores = pl.pallas_call(
        kernel,
        out_shape=jax.ShapeDtypeStruct((16, 16, 256), F32),
        in_specs=[any_spec, any_spec, vmem, vmem, vmem, vmem],
        out_specs=vmem,
        scratch_shapes=[
            pltpu.VMEM((8, 1024, 2, 128), BF16),
            pltpu.VMEM((2, 2, 512, 1024), BF16),
            pltpu.VMEM((4, 512, 2048), BF16),
            pltpu.VMEM((8, 2, 2, 8, 16, 128), BF16),
            pltpu.VMEM((8, 2, 2, 8, 16, 128), BF16),
            pltpu.VMEM((8, 8, 2, 64, 256), BF16),
            pltpu.VMEM((23, 2, 16, 256), F32),
            pltpu.VMEM((23, 16, 256), SENT),
            pltpu.VMEM((23, 16, 256), SENT),
            pltpu.VMEM((7, 16, 256), SENT),
            pltpu.VMEM((7, 16, 256), SENT),
            dma(()), dma(()), dma(()),
            dma(()), dma((8,)), dma((8,)),
            dma(()), dma(()), dma(()), dma(()), dma(()), dma(()),
            dma((8,)), dma((8,)), dma((8,)),
            dma((3,)), dma((3,)), dma(()), dma(()),
        ],
        compiler_params=pltpu.CompilerParams(
            collective_id=0, has_side_effects=True, vmem_limit_bytes=56 * 1024 * 1024
        ),
    )(spectra, steering, by_bin, *rows)
    return jnp.transpose(scores, (1, 0, 2))


def solution(mesh):
    return jax.shard_map(
        per_device,
        mesh=mesh,
        in_specs=(
            P("beam", "tm", None, None),
            P("beam", None, None, None),
            P(None, None, "beam"),
            P(),
            P(),
            P(),
        ),
        out_specs=P("beam", "tm", None),
        check_vma=False,
    )
```

```python
import jax
import jax.numpy as jnp
from jax import lax
from jax.experimental import pallas as pl
from jax.experimental.pallas import tpu as pltpu
from jax.sharding import PartitionSpec as P

MESH = pl.DeviceIdType.MESH
CHUNKS = 8
LAGS = 8
SEGMENTS = ((0, 8), (8, 6), (14, 4), (18, 5))
F32 = jnp.float32
BF16 = jnp.bfloat16
SENT = BF16


def kernel(
    spec, steer, tmpl, tlen, bst, bwd, out,
    tmpl_v, rows_v, m_own,
    xbuf, wst, wmix, ppow, pin, tbuf, acc, ssend, sbuf, hsend, hrecv,
    w_own, w_send, w_recv, x_own, x_send, x_recv, t_send, t_recv, y_send, y_recv, t2_send, t2_recv,
    p_own, p_send, p_recv, s_send, s_recv, h_send, h_recv,
):
    me = lax.axis_index("beam")
    tm = lax.axis_index("tm")
    core = me % 2
    sib = me + 1 - 2 * core
    half = me // 16
    local = me % 16
    kk = local // 2
    partner = (me + 16) % 32
    quarter = tm % 4

    def remote(src, dst, send_sem, recv_sem, beam, tm_index=None):
        return pltpu.make_async_remote_copy(
            src_ref=src, dst_ref=dst, send_sem=send_sem, recv_sem=recv_sem,
            device_id=(beam, tm if tm_index is None else tm_index), device_id_type=MESH,
        )

    def y_peer(off):
        return tm - quarter + (quarter + off) % 4

    def wait_bytes(ref, sem):
        pltpu.make_async_copy(ref, ref, sem).wait()

    def tile(device):
        return pl.ds(pl.multiple_of((device // 2) * 128, 128), 128)

    barrier = pltpu.get_barrier_semaphore()

    def greet(off, _):
        pl.semaphore_signal(barrier, inc=1, device_id=((me + off) % 32, tm), device_id_type=MESH)
        return 0

    lax.fori_loop(1, 32, greet, 0)
    for off in (1, 2, 3):
        pl.semaphore_signal(barrier, inc=1, device_id=(me, y_peer(off)), device_id_type=MESH)

    @pl.when((tm == 3) | (tm == 4))
    def _():
        pl.semaphore_signal(barrier, inc=1, device_id=(me, 7 - tm), device_id_type=MESH)

    own_w = pltpu.make_async_copy(steer.at[0], wst.at[core], w_own)
    own_w.start()
    own_t = pltpu.make_async_copy(tmpl.at[pl.ds(2 * quarter, 2)], tmpl_v, m_own.at[0])
    own_t.start()
    own_r = [
        pltpu.make_async_copy(a, rows_v.at[i], m_own.at[1 + i])
        for i, a in enumerate((tlen, bst, bwd))
    ]
    for c in own_r:
        c.start()

    def own_x(j, _):
        pltpu.make_async_copy(
            spec.at[:, 2 * j + core, :, tile(me)], xbuf.at[j, pl.ds(32 * me, 32)], x_own
        ).start()
        return 0

    lax.fori_loop(0, CHUNKS, own_x, 0)

    bins = 64 * me + lax.broadcasted_iota(jnp.int32, (64, 256), 0)
    own_t.wait()
    for c in own_r:
        c.wait()
    first = rows_v[1]
    keep = jnp.where((bins >= first) & (bins < first + rows_v[2]), 1, 0)
    length = jnp.broadcast_to(rows_v[0], (64, 256))
    for i in range(2):
        lag = 2 * quarter + i
        tbuf[lag, kk, core] = jnp.where(
            (keep == 1) & (length > lag), tmpl_v[i].astype(F32), 0.0
        ).astype(BF16)

    pl.semaphore_wait(barrier, 34 + jnp.where((tm == 3) | (tm == 4), 1, 0))

    w_copy = remote(steer.at[0], wst.at[core], w_send, w_recv, sib)
    w_copy.start()

    def send_t(off, _):
        part = tbuf.at[pl.ds(2 * quarter, 2), kk, core]
        remote(part, part, t_send, t_recv, 16 * half + (local + 2 * off) % 16).start()
        return 0


    def send_x(j):
        def body(off, _):
            peer = (16 * (1 - half) + (local + off) % 16 + 16 * (off // 16)) % 32
            remote(
                spec.at[:, 2 * j + peer % 2, :, tile(peer)],
                xbuf.at[j, pl.ds(32 * me, 32)],
                x_send.at[j], x_recv.at[j], peer,
            ).start()
            return 0

        lax.fori_loop(0, 16, body, 0)
        lax.fori_loop(17, 32, body, 0)

    send_x(0)
    lax.fori_loop(1, 8, send_t, 0)
    send_x(1)
    send_x(2)

    own_w.wait()
    w_copy.wait_recv()
    row = lax.broadcasted_iota(jnp.int32, (256, 256), 0)
    col = lax.broadcasted_iota(jnp.int32, (256, 256), 1)
    e_even = jnp.where((row < 128) & (col == 2 * row), 1.0, 0.0)
    odd = (row >= 128) & (col == 2 * (row - 128) + 1)
    e_real = (e_even - jnp.where(odd, 1.0, 0.0)).astype(BF16)
    i_even = (row >= 128) & (col == 2 * (row - 128))
    i_odd = (row < 128) & (col == 2 * row + 1)
    e_imag = jnp.where(i_even | i_odd, 1.0, 0.0).astype(BF16)

    def mix(n, _):
        s, cb = n // 8, n % 8
        cols = pl.ds(pl.multiple_of(cb * 128, 128), 128)
        both = jnp.concatenate([wst[s, 0, :, cols], wst[s, 1, :, cols]], axis=1)
        outcols = pl.ds(pl.multiple_of(cb * 256, 256), 256)
        for ri, e in enumerate((e_real, e_imag)):
            m = jnp.dot(both, e, preferred_element_type=F32).astype(BF16)
            rows = pl.ds(pl.multiple_of((s * 2 + ri) * 128, 128), 128)
            wmix[:, rows, outcols] = m.reshape(4, 128, 256)
        return 0

    lax.fori_loop(0, 16, mix, 0)
    acc[...] = jnp.zeros_like(acc)

    wait_bytes(tbuf.at[pl.ds(0, 2), pl.ds(0, 7), 0], t_recv)
    for off in (1, 2, 3):
        part = tbuf.at[pl.ds(2 * quarter, 2), :, core]
        remote(part, part, y_send, y_recv, me, y_peer(off)).start()

    xflat = xbuf.reshape(CHUNKS, 2048, 128)
    low = lax.broadcasted_iota(jnp.int32, (128, 128), 1) < 64

    def own_p(j):
        return pltpu.make_async_copy(
            ppow.at[j, :, local // 8, local % 8], pin.at[j, core, :, kk], p_own.at[j]
        )

    def power(j):
        wait_bytes(xbuf.at[0, pl.ds(0, 992)], x_recv.at[j])

        def block(zh, zl):
            b = 2 * zh + zl
            y = jnp.dot(wmix[b], xflat[j], preferred_element_type=F32)
            ar, ai, br, bi = y[0:128], y[128:256], y[256:384], y[384:512]
            p = jnp.where(low, ar * ar + ai * ai, br * br + bi * bi).astype(BF16)
            ppow[j, zh, zl] = p.reshape(8, 16, 128)
            return zl

        def send_p(off, far):
            q = 8 * ((local // 8 + far) % 2) + (local + off) % 8
            remote(
                ppow.at[j, :, q // 8, q % 8], pin.at[j, core, :, kk],
                p_send.at[j], p_recv.at[j], 16 * half + q,
            ).start()
            return far

        lax.fori_loop(0, 2, block, 1 - local // 8)
        lax.fori_loop(0, 8, send_p, 1)
        lax.fori_loop(0, 2, block, local // 8)
        own_p(j).start()
        lax.fori_loop(1, 8, send_p, 0)

    def arrived(j):
        own_p(j).wait()
        wait_bytes(xbuf.at[0, pl.ds(0, 240)], p_recv.at[j])

    def correlate(j, start=0, stop=LAGS):
        def lag_step(step, _):
            lag = LAGS - 1 - step
            parts = [pin[j, :, :, k].reshape(64, 128) for k in range(8)]
            lhs = jnp.concatenate(parts, axis=1)
            w = tbuf[lag].reshape(1024, 256)
            res = jnp.dot(lhs, w, preferred_element_type=F32).reshape(2, 2, 16, 256)
            rows = pl.ds(2 * j + 7 - lag, 2)
            acc[rows] = acc[rows] + res
            return 0

        lax.fori_loop(start, stop, lag_step, 0)

    def score_copy(g):
        rows = pl.ds(*SEGMENTS[g])
        return remote(ssend.at[rows], sbuf.at[rows], s_send.at[g], s_recv.at[g], partner)

    def send_scores(g):
        rows = pl.ds(*SEGMENTS[g])
        ssend[rows] = acc[rows, 1 - half].astype(SENT)
        score_copy(g).start()

    t2 = remote(tbuf.at[:, :, core], tbuf.at[:, :, core], t2_send, t2_recv, sib)
    h_copy = remote(hsend, hrecv, h_send, h_recv, me, tm - 1)

    wait_bytes(xbuf.at[pl.ds(0, CHUNKS), pl.ds(0, 32)], x_own)
    power(0)
    send_x(3)
    power(1)
    send_x(4)
    power(2)
    send_x(5)
    wait_bytes(tbuf.at[pl.ds(0, 6), :, 0], y_recv)
    t2.start()
    power(3)
    send_x(6)
    t2.wait_recv()
    arrived(0)
    correlate(0)
    arrived(1)
    correlate(1)
    power(4)
    send_x(7)
    arrived(2)
    correlate(2)
    arrived(3)
    correlate(3)
    send_scores(0)
    power(5)
    arrived(4)
    correlate(4)
    power(6)
    arrived(5)
    correlate(5)

    score_copy(0).wait_recv()

    @pl.when(tm > 0)
    def _():
        hsend[...] = (acc[0:7, half] + sbuf[0:7].astype(F32)).astype(SENT)
        h_copy.start()

    power(7)
    arrived(6)
    correlate(6)
    send_scores(1)
    arrived(7)
    correlate(7, 0, 4)
    send_scores(2)
    correlate(7, 4, 8)
    send_scores(3)
    score_copy(1).wait_recv()
    score_copy(2).wait_recv()
    score_copy(3).wait_recv()
    out[...] = acc[7:23, half] + sbuf[7:23].astype(F32)

    @pl.when(tm < 7)
    def _():
        h_copy.wait_recv()
        out[9:16] = out[9:16] + hrecv[...].astype(F32)

    w_copy.wait_send()
    t2.wait_send()
    wait_bytes(tbuf.at[pl.ds(0, 2), pl.ds(0, 7), 0], t_send)
    wait_bytes(tbuf.at[pl.ds(0, 6), :, 0], y_send)
    for j in range(CHUNKS):
        wait_bytes(xbuf.at[0, pl.ds(0, 992)], x_send.at[j])
        wait_bytes(xbuf.at[0, pl.ds(0, 240)], p_send.at[j])
    for g in range(4):
        score_copy(g).wait_send()

    @pl.when(tm > 0)
    def _():
        h_copy.wait_send()


def per_device(spectra, steering, templates, tmpl_length, band_start, band_width):
    rows = [a.reshape(1, -1) for a in (tmpl_length, band_start, band_width)]
    by_bin = jnp.transpose(templates, (1, 2, 0))
    any_spec = pl.BlockSpec(memory_space=pl.ANY)
    vmem = pl.BlockSpec(memory_space=pltpu.VMEM)
    dma = pltpu.SemaphoreType.DMA
    scores = pl.pallas_call(
        kernel,
        out_shape=jax.ShapeDtypeStruct((16, 16, 256), F32),
        in_specs=[any_spec] * 6,
        out_specs=vmem,
        scratch_shapes=[
            pltpu.VMEM((2, 64, 256), BF16),
            pltpu.VMEM((3, 1, 256), jnp.int32),
            dma((4,)),
            pltpu.VMEM((8, 1024, 2, 128), BF16),
            pltpu.VMEM((2, 2, 512, 1024), BF16),
            pltpu.VMEM((4, 512, 2048), BF16),
            pltpu.VMEM((8, 2, 2, 8, 16, 128), BF16),
            pltpu.VMEM((8, 2, 2, 8, 16, 128), BF16),
            pltpu.VMEM((8, 8, 2, 64, 256), BF16),
            pltpu.VMEM((23, 2, 16, 256), F32),
            pltpu.VMEM((23, 16, 256), SENT),
            pltpu.VMEM((23, 16, 256), SENT),
            pltpu.VMEM((7, 16, 256), SENT),
            pltpu.VMEM((7, 16, 256), SENT),
            dma(()), dma(()), dma(()),
            dma(()), dma((8,)), dma((8,)),
            dma(()), dma(()), dma(()), dma(()), dma(()), dma(()),
            dma((8,)), dma((8,)), dma((8,)),
            dma((4,)), dma((4,)), dma(()), dma(()),
        ],
        compiler_params=pltpu.CompilerParams(
            collective_id=0, has_side_effects=True, vmem_limit_bytes=56 * 1024 * 1024
        ),
    )(spectra, steering, by_bin, *rows)
    return jnp.transpose(scores, (1, 0, 2))


def solution(mesh):
    return jax.shard_map(
        per_device,
        mesh=mesh,
        in_specs=(
            P("beam", "tm", None, None),
            P("beam", None, None, None),
            P(None, None, "beam"),
            P(),
            P(),
            P(),
        ),
        out_specs=P("beam", "tm", None),
        check_vma=False,
    )
```

```python
import jax
import jax.numpy as jnp
from jax import lax
from jax.experimental import pallas as pl
from jax.experimental.pallas import tpu as pltpu
from jax.sharding import PartitionSpec as P

MESH = pl.DeviceIdType.MESH
CHUNKS = 8
LAGS = 8
SEGMENTS = ((0, 8), (8, 6), (14, 4), (18, 5))
F32 = jnp.float32
BF16 = jnp.bfloat16
SENT = BF16


def kernel(
    spec, steer, tmpl, tlen, bst, bwd, out,
    tmpl_v, rows_v, m_own, rounds, tell_sem,
    xbuf, wst, wmix, ppow, pin, tbuf, acc, ssend, sbuf, hsend, hrecv,
    w_own, w_send, w_recv, x_own, x_send, x_recv, t_send, t_recv, y_send, y_recv, t2_send, t2_recv,
    p_own, p_send, p_recv, s_send, s_recv, h_send, h_recv,
):
    me = lax.axis_index("beam")
    tm = lax.axis_index("tm")
    core = me % 2
    sib = me + 1 - 2 * core
    half = me // 16
    local = me % 16
    kk = local // 2
    partner = (me + 16) % 32
    quarter = tm % 4

    def remote(src, dst, send_sem, recv_sem, beam, tm_index=None):
        return pltpu.make_async_remote_copy(
            src_ref=src, dst_ref=dst, send_sem=send_sem, recv_sem=recv_sem,
            device_id=(beam, tm if tm_index is None else tm_index), device_id_type=MESH,
        )

    def y_peer(off):
        return tm - quarter + (quarter + off) % 4

    def wait_bytes(ref, sem):
        pltpu.make_async_copy(ref, ref, sem).wait()

    def tile(device):
        return pl.ds(pl.multiple_of((device // 2) * 128, 128), 128)

    barrier = pltpu.get_barrier_semaphore()

    row = me // 8
    sides = 2 - jnp.where((row == 0) | (row == 3), 1, 0)

    def signal(sem, beam, tm_index):
        pl.semaphore_signal(sem, inc=1, device_id=(beam, tm_index), device_id_type=MESH)

    def greet_rows(sem):
        @pl.when(row < 3)
        def _():
            signal(sem, me + 8, tm)

        @pl.when(row > 0)
        def _():
            signal(sem, me - 8, tm)

    greet_rows(barrier)

    def greet(off, _):
        signal(barrier, 8 * row + (me + off) % 8, tm)
        return 0

    lax.fori_loop(1, 8, greet, 0)
    for off in (1, 2, 3):
        signal(barrier, me, y_peer(off))

    teller = (tm == 0) & (row == 3)
    told = (tm == 4) & (row == 0)

    @pl.when(teller)
    def _():
        signal(barrier, me - 24, 4)

    @pl.when(told)
    def _():
        signal(barrier, me + 24, 0)

    own_w = pltpu.make_async_copy(steer.at[0], wst.at[core], w_own)
    own_w.start()
    own_t = pltpu.make_async_copy(tmpl.at[pl.ds(2 * quarter, 2)], tmpl_v, m_own.at[0])
    own_t.start()
    own_r = [
        pltpu.make_async_copy(a, rows_v.at[i], m_own.at[1 + i])
        for i, a in enumerate((tlen, bst, bwd))
    ]
    for c in own_r:
        c.start()

    def own_x(j, _):
        pltpu.make_async_copy(
            spec.at[:, 2 * j + core, :, tile(me)], xbuf.at[j, pl.ds(32 * me, 32)], x_own
        ).start()
        return 0

    lax.fori_loop(0, CHUNKS, own_x, 0)

    bins = 64 * me + lax.broadcasted_iota(jnp.int32, (64, 256), 0)
    own_t.wait()
    for c in own_r:
        c.wait()
    first = rows_v[1]
    keep = jnp.where((bins >= first) & (bins < first + rows_v[2]), 1, 0)
    length = jnp.broadcast_to(rows_v[0], (64, 256))
    for i in range(2):
        lag = 2 * quarter + i
        tbuf[lag, kk, core] = jnp.where(
            (keep == 1) & (length > lag), tmpl_v[i].astype(F32), 0.0
        ).astype(BF16)

    pl.semaphore_wait(barrier, 10 + sides + jnp.where(teller | told, 1, 0))
    greet_rows(rounds.at[0])

    w_copy = remote(steer.at[0], wst.at[core], w_send, w_recv, sib)
    w_copy.start()

    def send_t(off, _):
        part = tbuf.at[pl.ds(2 * quarter, 2), kk, core]
        remote(part, part, t_send, t_recv, 16 * half + (local + 2 * off) % 16).start()
        return 0


    def send_row(away, start):
        def body(off, _):
            peer = 8 * (row + away) + (me + off) % 8
            remote(
                spec.at[:, peer % 2, :, tile(peer)], xbuf.at[0, pl.ds(32 * me, 32)],
                x_send.at[0], x_recv.at[0], peer,
            ).start()
            return 0

        lax.fori_loop(start, 8, body, 0)

    def send_x(j):
        def body(off, _):
            peer = (16 * (1 - half) + (local + off) % 16 + 16 * (off // 16)) % 32
            remote(
                spec.at[:, 2 * j + peer % 2, :, tile(peer)],
                xbuf.at[j, pl.ds(32 * me, 32)],
                x_send.at[j], x_recv.at[j], peer,
            ).start()
            return 0

        lax.fori_loop(0, 16, body, 0)
        lax.fori_loop(17, 32, body, 0)

    send_row(0, 1)
    for far in (1, 2, 3):
        pl.semaphore_wait(rounds.at[far - 1], sides)
        if far < 3:
            greet_rows(rounds.at[far])

        @pl.when(row + far < 4)
        def _():
            send_row(far, 0)

        @pl.when(row >= far)
        def _():
            send_row(-far, 0)

    lax.fori_loop(1, 8, send_t, 0)
    send_x(1)
    send_x(2)

    own_w.wait()
    w_copy.wait_recv()
    line = lax.broadcasted_iota(jnp.int32, (256, 256), 0)
    col = lax.broadcasted_iota(jnp.int32, (256, 256), 1)
    e_even = jnp.where((line < 128) & (col == 2 * line), 1.0, 0.0)
    odd = (line >= 128) & (col == 2 * (line - 128) + 1)
    e_real = (e_even - jnp.where(odd, 1.0, 0.0)).astype(BF16)
    i_even = (line >= 128) & (col == 2 * (line - 128))
    i_odd = (line < 128) & (col == 2 * line + 1)
    e_imag = jnp.where(i_even | i_odd, 1.0, 0.0).astype(BF16)

    def mix(n, _):
        s, cb = n // 8, n % 8
        cols = pl.ds(pl.multiple_of(cb * 128, 128), 128)
        both = jnp.concatenate([wst[s, 0, :, cols], wst[s, 1, :, cols]], axis=1)
        outcols = pl.ds(pl.multiple_of(cb * 256, 256), 256)
        for ri, e in enumerate((e_real, e_imag)):
            m = jnp.dot(both, e, preferred_element_type=F32).astype(BF16)
            rows = pl.ds(pl.multiple_of((s * 2 + ri) * 128, 128), 128)
            wmix[:, rows, outcols] = m.reshape(4, 128, 256)
        return 0

    lax.fori_loop(0, 16, mix, 0)
    acc[...] = jnp.zeros_like(acc)

    wait_bytes(tbuf.at[pl.ds(0, 2), pl.ds(0, 7), 0], t_recv)
    for off in (1, 2, 3):
        part = tbuf.at[pl.ds(2 * quarter, 2), :, core]
        remote(part, part, y_send, y_recv, me, y_peer(off)).start()

    xflat = xbuf.reshape(CHUNKS, 2048, 128)
    low = lax.broadcasted_iota(jnp.int32, (128, 128), 1) < 64

    def own_p(j):
        return pltpu.make_async_copy(
            ppow.at[j, :, local // 8, local % 8], pin.at[j, core, :, kk], p_own.at[j]
        )

    def power(j):
        wait_bytes(xbuf.at[0, pl.ds(0, 992)], x_recv.at[j])

        def block(zh, zl):
            b = 2 * zh + zl
            y = jnp.dot(wmix[b], xflat[j], preferred_element_type=F32)
            ar, ai, br, bi = y[0:128], y[128:256], y[256:384], y[384:512]
            p = jnp.where(low, ar * ar + ai * ai, br * br + bi * bi).astype(BF16)
            ppow[j, zh, zl] = p.reshape(8, 16, 128)
            return zl

        def send_p(off, far):
            q = 8 * ((local // 8 + far) % 2) + (local + off) % 8
            remote(
                ppow.at[j, :, q // 8, q % 8], pin.at[j, core, :, kk],
                p_send.at[j], p_recv.at[j], 16 * half + q,
            ).start()
            return far

        lax.fori_loop(0, 2, block, 1 - local // 8)
        lax.fori_loop(0, 8, send_p, 1)
        lax.fori_loop(0, 2, block, local // 8)
        own_p(j).start()
        lax.fori_loop(1, 8, send_p, 0)

    def arrived(j):
        own_p(j).wait()
        wait_bytes(xbuf.at[0, pl.ds(0, 240)], p_recv.at[j])

    def correlate(j, start=0, stop=LAGS):
        def lag_step(step, _):
            lag = LAGS - 1 - step
            parts = [pin[j, :, :, k].reshape(64, 128) for k in range(8)]
            lhs = jnp.concatenate(parts, axis=1)
            w = tbuf[lag].reshape(1024, 256)
            res = jnp.dot(lhs, w, preferred_element_type=F32).reshape(2, 2, 16, 256)
            rows = pl.ds(2 * j + 7 - lag, 2)
            acc[rows] = acc[rows] + res
            return 0

        lax.fori_loop(start, stop, lag_step, 0)

    def score_copy(g):
        rows = pl.ds(*SEGMENTS[g])
        return remote(ssend.at[rows], sbuf.at[rows], s_send.at[g], s_recv.at[g], partner)

    def send_scores(g):
        rows = pl.ds(*SEGMENTS[g])
        ssend[rows] = acc[rows, 1 - half].astype(SENT)
        score_copy(g).start()

    t2 = remote(tbuf.at[:, :, core], tbuf.at[:, :, core], t2_send, t2_recv, sib)
    h_copy = remote(hsend, hrecv, h_send, h_recv, me, tm - 1)

    wait_bytes(xbuf.at[pl.ds(0, CHUNKS), pl.ds(0, 32)], x_own)
    power(0)

    @pl.when(teller)
    def _():
        signal(tell_sem, me - 24, 4)

    send_x(3)
    power(1)
    send_x(4)
    power(2)
    send_x(5)
    wait_bytes(tbuf.at[pl.ds(0, 6), :, 0], y_recv)
    t2.start()
    @pl.when(told)
    def _():
        pl.semaphore_wait(tell_sem, 1)

    power(3)
    send_x(6)
    t2.wait_recv()
    arrived(0)
    correlate(0)
    arrived(1)
    correlate(1)
    power(4)
    send_x(7)
    arrived(2)
    correlate(2)
    arrived(3)
    correlate(3)
    send_scores(0)
    power(5)
    arrived(4)
    correlate(4)
    power(6)
    arrived(5)
    correlate(5)

    power(7)

    score_copy(0).wait_recv()

    @pl.when(tm > 0)
    def _():
        hsend[...] = (acc[0:7, half] + sbuf[0:7].astype(F32)).astype(SENT)
        h_copy.start()

    arrived(6)
    correlate(6)
    send_scores(1)
    arrived(7)
    correlate(7, 0, 4)
    send_scores(2)
    correlate(7, 4, 8)
    send_scores(3)
    score_copy(1).wait_recv()
    score_copy(2).wait_recv()
    score_copy(3).wait_recv()
    out[...] = acc[7:23, half] + sbuf[7:23].astype(F32)

    @pl.when(tm < 7)
    def _():
        h_copy.wait_recv()
        out[9:16] = out[9:16] + hrecv[...].astype(F32)

    w_copy.wait_send()
    t2.wait_send()
    wait_bytes(tbuf.at[pl.ds(0, 2), pl.ds(0, 7), 0], t_send)
    wait_bytes(tbuf.at[pl.ds(0, 6), :, 0], y_send)
    for j in range(CHUNKS):
        wait_bytes(xbuf.at[0, pl.ds(0, 992)], x_send.at[j])
        wait_bytes(xbuf.at[0, pl.ds(0, 240)], p_send.at[j])
    for g in range(4):
        score_copy(g).wait_send()

    @pl.when(tm > 0)
    def _():
        h_copy.wait_send()


def per_device(spectra, steering, templates, tmpl_length, band_start, band_width):
    rows = [a.reshape(1, -1) for a in (tmpl_length, band_start, band_width)]
    by_bin = jnp.transpose(templates, (1, 2, 0))
    any_spec = pl.BlockSpec(memory_space=pl.ANY)
    vmem = pl.BlockSpec(memory_space=pltpu.VMEM)
    dma = pltpu.SemaphoreType.DMA
    scores = pl.pallas_call(
        kernel,
        out_shape=jax.ShapeDtypeStruct((16, 16, 256), F32),
        in_specs=[any_spec] * 6,
        out_specs=vmem,
        scratch_shapes=[
            pltpu.VMEM((2, 64, 256), BF16),
            pltpu.VMEM((3, 1, 256), jnp.int32),
            dma((4,)),
            pltpu.SemaphoreType.REGULAR((3,)),
            pltpu.SemaphoreType.REGULAR,
            pltpu.VMEM((8, 1024, 2, 128), BF16),
            pltpu.VMEM((2, 2, 512, 1024), BF16),
            pltpu.VMEM((4, 512, 2048), BF16),
            pltpu.VMEM((8, 2, 2, 8, 16, 128), BF16),
            pltpu.VMEM((8, 2, 2, 8, 16, 128), BF16),
            pltpu.VMEM((8, 8, 2, 64, 256), BF16),
            pltpu.VMEM((23, 2, 16, 256), F32),
            pltpu.VMEM((23, 16, 256), SENT),
            pltpu.VMEM((23, 16, 256), SENT),
            pltpu.VMEM((7, 16, 256), SENT),
            pltpu.VMEM((7, 16, 256), SENT),
            dma(()), dma(()), dma(()),
            dma(()), dma((8,)), dma((8,)),
            dma(()), dma(()), dma(()), dma(()), dma(()), dma(()),
            dma((8,)), dma((8,)), dma((8,)),
            dma((4,)), dma((4,)), dma(()), dma(()),
        ],
        compiler_params=pltpu.CompilerParams(
            collective_id=0, has_side_effects=True, vmem_limit_bytes=56 * 1024 * 1024
        ),
    )(spectra, steering, by_bin, *rows)
    return jnp.transpose(scores, (1, 0, 2))


def solution(mesh):
    return jax.shard_map(
        per_device,
        mesh=mesh,
        in_specs=(
            P("beam", "tm", None, None),
            P("beam", None, None, None),
            P(None, None, "beam"),
            P(),
            P(),
            P(),
        ),
        out_specs=P("beam", "tm", None),
        check_vma=False,
    )
```

```python
import jax
import jax.numpy as jnp
from jax import lax
from jax.experimental import pallas as pl
from jax.experimental.pallas import tpu as pltpu
from jax.sharding import PartitionSpec as P

MESH = pl.DeviceIdType.MESH
CHUNKS = 8
LAGS = 8
SEGMENTS = ((0, 8), (8, 6), (14, 4), (18, 5))
F32 = jnp.float32
BF16 = jnp.bfloat16
SENT = BF16


def kernel(
    spec, steer, tmpl, tlen, bst, bwd, out,
    tmpl_v, rows_v, m_own, rounds, tell_sem,
    xbuf, wst, wmix, ppow, pin, tbuf, acc, ssend, sbuf, hsend, hrecv,
    w_own, w_send, w_recv, x_own, x_send, x_recv, t_send, t_recv, y_send, y_recv, t2_send, t2_recv,
    p_own, p_send, p_recv, s_send, s_recv, h_send, h_recv,
):
    me = lax.axis_index("beam")
    tm = lax.axis_index("tm")
    core = me % 2
    sib = me + 1 - 2 * core
    half = me // 16
    local = me % 16
    kk = local // 2
    partner = (me + 16) % 32
    quarter = tm % 4

    def remote(src, dst, send_sem, recv_sem, beam, tm_index=None):
        return pltpu.make_async_remote_copy(
            src_ref=src, dst_ref=dst, send_sem=send_sem, recv_sem=recv_sem,
            device_id=(beam, tm if tm_index is None else tm_index), device_id_type=MESH,
        )

    def y_peer(off):
        return tm - quarter + (quarter + off) % 4

    def wait_bytes(ref, sem):
        pltpu.make_async_copy(ref, ref, sem).wait()

    def tile(device):
        return pl.ds(pl.multiple_of((device // 2) * 128, 128), 128)

    barrier = pltpu.get_barrier_semaphore()

    row = me // 8
    sides = 2 - jnp.where((row == 0) | (row == 3), 1, 0)

    def signal(sem, beam, tm_index):
        pl.semaphore_signal(sem, inc=1, device_id=(beam, tm_index), device_id_type=MESH)

    def greet_rows(sem):
        @pl.when(row < 3)
        def _():
            signal(sem, me + 8, tm)

        @pl.when(row > 0)
        def _():
            signal(sem, me - 8, tm)

    greet_rows(barrier)

    def greet(off, _):
        signal(barrier, 8 * row + (me + off) % 8, tm)
        return 0

    lax.fori_loop(1, 8, greet, 0)
    for off in (1, 2, 3):
        signal(barrier, me, y_peer(off))

    teller = (tm == 0) & (row == 3)
    told = (tm == 4) & (row == 0)

    @pl.when(teller)
    def _():
        signal(barrier, me - 24, 4)

    @pl.when(told)
    def _():
        signal(barrier, me + 24, 0)

    own_w = pltpu.make_async_copy(steer.at[0], wst.at[core], w_own)
    own_w.start()
    own_t = pltpu.make_async_copy(tmpl.at[pl.ds(2 * quarter, 2)], tmpl_v, m_own.at[0])
    own_t.start()
    own_r = [
        pltpu.make_async_copy(a, rows_v.at[i], m_own.at[1 + i])
        for i, a in enumerate((tlen, bst, bwd))
    ]
    for c in own_r:
        c.start()

    def own_x(j, _):
        pltpu.make_async_copy(
            spec.at[:, 2 * j + core, :, tile(me)], xbuf.at[j, pl.ds(32 * me, 32)], x_own
        ).start()
        return 0

    lax.fori_loop(0, CHUNKS, own_x, 0)

    bins = 64 * me + lax.broadcasted_iota(jnp.int32, (64, 256), 0)
    own_t.wait()
    for c in own_r:
        c.wait()
    first = rows_v[1]
    keep = jnp.where((bins >= first) & (bins < first + rows_v[2]), 1, 0)
    length = jnp.broadcast_to(rows_v[0], (64, 256))
    for i in range(2):
        lag = 2 * quarter + i
        tbuf[lag, kk, core] = jnp.where(
            (keep == 1) & (length > lag), tmpl_v[i].astype(F32), 0.0
        ).astype(BF16)

    pl.semaphore_wait(barrier, 10 + sides + jnp.where(teller | told, 1, 0))
    greet_rows(rounds.at[0])

    w_copy = remote(steer.at[0], wst.at[core], w_send, w_recv, sib)
    w_copy.start()

    def send_t(off, _):
        part = tbuf.at[pl.ds(2 * quarter, 2), kk, core]
        remote(part, part, t_send, t_recv, 16 * half + (local + 2 * off) % 16).start()
        return 0


    def send_row(away, start):
        def body(off, _):
            peer = 8 * (row + away) + (me + off) % 8
            remote(
                spec.at[:, peer % 2, :, tile(peer)], xbuf.at[0, pl.ds(32 * me, 32)],
                x_send.at[0], x_recv.at[0], peer,
            ).start()
            return 0

        lax.fori_loop(start, 8, body, 0)

    def send_x(j):
        def body(off, _):
            peer = (16 * (1 - half) + (local + off) % 16 + 16 * (off // 16)) % 32
            remote(
                spec.at[:, 2 * j + peer % 2, :, tile(peer)],
                xbuf.at[j, pl.ds(32 * me, 32)],
                x_send.at[j], x_recv.at[j], peer,
            ).start()
            return 0

        lax.fori_loop(0, 16, body, 0)
        lax.fori_loop(17, 32, body, 0)

    send_row(0, 1)
    for far in (1, 2, 3):
        pl.semaphore_wait(rounds.at[far - 1], sides)
        if far < 3:
            greet_rows(rounds.at[far])

        @pl.when(row + far < 4)
        def _():
            send_row(far, 0)

        @pl.when(row >= far)
        def _():
            send_row(-far, 0)

    lax.fori_loop(1, 8, send_t, 0)
    send_x(1)
    send_x(2)

    own_w.wait()
    w_copy.wait_recv()
    line = lax.broadcasted_iota(jnp.int32, (256, 256), 0)
    col = lax.broadcasted_iota(jnp.int32, (256, 256), 1)
    e_even = jnp.where((line < 128) & (col == 2 * line), 1.0, 0.0)
    odd = (line >= 128) & (col == 2 * (line - 128) + 1)
    e_real = (e_even - jnp.where(odd, 1.0, 0.0)).astype(BF16)
    i_even = (line >= 128) & (col == 2 * (line - 128))
    i_odd = (line < 128) & (col == 2 * line + 1)
    e_imag = jnp.where(i_even | i_odd, 1.0, 0.0).astype(BF16)

    def mix(n, _):
        s, cb = n // 8, n % 8
        cols = pl.ds(pl.multiple_of(cb * 128, 128), 128)
        both = jnp.concatenate([wst[s, 0, :, cols], wst[s, 1, :, cols]], axis=1)
        outcols = pl.ds(pl.multiple_of(cb * 256, 256), 256)
        for ri, e in enumerate((e_real, e_imag)):
            m = jnp.dot(both, e, preferred_element_type=F32).astype(BF16)
            rows = pl.ds(pl.multiple_of((s * 2 + ri) * 128, 128), 128)
            wmix[:, rows, outcols] = m.reshape(4, 128, 256)
        return 0

    lax.fori_loop(0, 16, mix, 0)
    acc[...] = jnp.zeros_like(acc)

    wait_bytes(tbuf.at[pl.ds(0, 2), pl.ds(0, 7), 0], t_recv)
    for off in (1, 2, 3):
        part = tbuf.at[pl.ds(2 * quarter, 2), :, core]
        remote(part, part, y_send, y_recv, me, y_peer(off)).start()

    xflat = xbuf.reshape(CHUNKS, 2048, 128)
    low = lax.broadcasted_iota(jnp.int32, (128, 128), 1) < 64

    def own_p(j):
        return pltpu.make_async_copy(
            ppow.at[j, :, local // 8, local % 8], pin.at[j, core, :, kk], p_own.at[j]
        )

    def power(j):
        wait_bytes(xbuf.at[0, pl.ds(0, 992)], x_recv.at[j])

        def block(zh, zl):
            b = 2 * zh + zl
            y = jnp.dot(wmix[b], xflat[j], preferred_element_type=F32)
            ar, ai, br, bi = y[0:128], y[128:256], y[256:384], y[384:512]
            p = jnp.where(low, ar * ar + ai * ai, br * br + bi * bi).astype(BF16)
            ppow[j, zh, zl] = p.reshape(8, 16, 128)
            return zl

        def send_p(off, far):
            q = 8 * ((local // 8 + far) % 2) + (local + off) % 8
            remote(
                ppow.at[j, :, q // 8, q % 8], pin.at[j, core, :, kk],
                p_send.at[j], p_recv.at[j], 16 * half + q,
            ).start()
            return far

        lax.fori_loop(0, 2, block, 1 - local // 8, unroll=j >= 7)
        lax.fori_loop(0, 8, send_p, 1)
        lax.fori_loop(0, 2, block, local // 8, unroll=j >= 7)
        own_p(j).start()
        lax.fori_loop(1, 8, send_p, 0)

    def arrived(j):
        own_p(j).wait()
        wait_bytes(xbuf.at[0, pl.ds(0, 240)], p_recv.at[j])

    def correlate(j, start=0, stop=LAGS):
        def lag_step(step, _):
            lag = LAGS - 1 - step
            parts = [pin[j, :, :, k].reshape(64, 128) for k in range(8)]
            lhs = jnp.concatenate(parts, axis=1)
            w = tbuf[lag].reshape(1024, 256)
            res = jnp.dot(lhs, w, preferred_element_type=F32).reshape(2, 2, 16, 256)
            rows = pl.ds(2 * j + 7 - lag, 2)
            acc[rows] = acc[rows] + res
            return 0

        lax.fori_loop(start, stop, lag_step, 0, unroll=j >= 6)

    def score_copy(g):
        rows = pl.ds(*SEGMENTS[g])
        return remote(ssend.at[rows], sbuf.at[rows], s_send.at[g], s_recv.at[g], partner)

    def send_scores(g):
        rows = pl.ds(*SEGMENTS[g])
        ssend[rows] = acc[rows, 1 - half].astype(SENT)
        score_copy(g).start()

    t2 = remote(tbuf.at[:, :, core], tbuf.at[:, :, core], t2_send, t2_recv, sib)
    h_copy = remote(hsend, hrecv, h_send, h_recv, me, tm - 1)

    wait_bytes(xbuf.at[pl.ds(0, CHUNKS), pl.ds(0, 32)], x_own)
    power(0)

    @pl.when(teller)
    def _():
        signal(tell_sem, me - 24, 4)

    send_x(3)
    power(1)
    send_x(4)
    power(2)
    send_x(5)
    wait_bytes(tbuf.at[pl.ds(0, 6), :, 0], y_recv)
    t2.start()
    @pl.when(told)
    def _():
        pl.semaphore_wait(tell_sem, 1)

    power(3)
    send_x(6)
    t2.wait_recv()
    arrived(0)
    correlate(0)
    arrived(1)
    correlate(1)
    power(4)
    send_x(7)
    arrived(2)
    correlate(2)
    arrived(3)
    correlate(3)
    send_scores(0)
    power(5)
    arrived(4)
    correlate(4)
    power(6)
    arrived(5)
    correlate(5)

    power(7)

    score_copy(0).wait_recv()

    @pl.when(tm > 0)
    def _():
        hsend[...] = (acc[0:7, half] + sbuf[0:7].astype(F32)).astype(SENT)
        h_copy.start()

    arrived(6)
    correlate(6)
    send_scores(1)
    arrived(7)
    correlate(7, 0, 4)
    send_scores(2)
    correlate(7, 4, 8)
    send_scores(3)
    score_copy(1).wait_recv()
    score_copy(2).wait_recv()
    score_copy(3).wait_recv()
    out[...] = acc[7:23, half] + sbuf[7:23].astype(F32)

    @pl.when(tm < 7)
    def _():
        h_copy.wait_recv()
        out[9:16] = out[9:16] + hrecv[...].astype(F32)

    w_copy.wait_send()
    t2.wait_send()
    wait_bytes(tbuf.at[pl.ds(0, 2), pl.ds(0, 7), 0], t_send)
    wait_bytes(tbuf.at[pl.ds(0, 6), :, 0], y_send)
    for j in range(CHUNKS):
        wait_bytes(xbuf.at[0, pl.ds(0, 992)], x_send.at[j])
        wait_bytes(xbuf.at[0, pl.ds(0, 240)], p_send.at[j])
    for g in range(4):
        score_copy(g).wait_send()

    @pl.when(tm > 0)
    def _():
        h_copy.wait_send()


def per_device(spectra, steering, templates, tmpl_length, band_start, band_width):
    rows = [a.reshape(1, -1) for a in (tmpl_length, band_start, band_width)]
    by_bin = jnp.transpose(templates, (1, 2, 0))
    any_spec = pl.BlockSpec(memory_space=pl.ANY)
    vmem = pl.BlockSpec(memory_space=pltpu.VMEM)
    dma = pltpu.SemaphoreType.DMA
    scores = pl.pallas_call(
        kernel,
        out_shape=jax.ShapeDtypeStruct((16, 16, 256), F32),
        in_specs=[any_spec] * 6,
        out_specs=vmem,
        scratch_shapes=[
            pltpu.VMEM((2, 64, 256), BF16),
            pltpu.VMEM((3, 1, 256), jnp.int32),
            dma((4,)),
            pltpu.SemaphoreType.REGULAR((3,)),
            pltpu.SemaphoreType.REGULAR,
            pltpu.VMEM((8, 1024, 2, 128), BF16),
            pltpu.VMEM((2, 2, 512, 1024), BF16),
            pltpu.VMEM((4, 512, 2048), BF16),
            pltpu.VMEM((8, 2, 2, 8, 16, 128), BF16),
            pltpu.VMEM((8, 2, 2, 8, 16, 128), BF16),
            pltpu.VMEM((8, 8, 2, 64, 256), BF16),
            pltpu.VMEM((23, 2, 16, 256), F32),
            pltpu.VMEM((23, 16, 256), SENT),
            pltpu.VMEM((23, 16, 256), SENT),
            pltpu.VMEM((7, 16, 256), SENT),
            pltpu.VMEM((7, 16, 256), SENT),
            dma(()), dma(()), dma(()),
            dma(()), dma((8,)), dma((8,)),
            dma(()), dma(()), dma(()), dma(()), dma(()), dma(()),
            dma((8,)), dma((8,)), dma((8,)),
            dma((4,)), dma((4,)), dma(()), dma(()),
        ],
        compiler_params=pltpu.CompilerParams(
            collective_id=0, has_side_effects=True, vmem_limit_bytes=56 * 1024 * 1024
        ),
    )(spectra, steering, by_bin, *rows)
    return jnp.transpose(scores, (1, 0, 2))


def solution(mesh):
    return jax.shard_map(
        per_device,
        mesh=mesh,
        in_specs=(
            P("beam", "tm", None, None),
            P("beam", None, None, None),
            P(None, None, "beam"),
            P(),
            P(),
            P(),
        ),
        out_specs=P("beam", "tm", None),
        check_vma=False,
    )
```
